32 devices in a mesh: sta: 16 (over z, x, core), tm: 2 (over y).
Axes of the slice: x: 2, y: 2, z: 4, core: 2. Of those that a mesh axis runs over, the one named last changes fastest.
Arguments:
- spectra: float32 [2, 64, 512, 256], P(None, 'tm', 'sta'), may hold values from -6 to 6
- valid: int32 [64, 512], P('tm', 'sta'), may hold values 0 or 1
Outputs:
- stacks: float32 [2, 4, 512, 32, 256], P(None, None, 'sta', 'tm')
The draws below stay inside these ranges and needn't reach their ends.
All inputs are finite; a program needn't handle non-finite values. No bound on the sum of `valid` on one device may be relied on, other than what follows from the above.
Results may differ from the reference program's by a relative error of at most 0.0001.
Values sent between devices are 32-bit elements; how exact they have to be, the bound alone decides.
A program may use at most 192 MiB of HBM per device.

```python
import jax
import jax.numpy as jnp
from jax import lax

F = 256
STA_DEV = 32
OFFSETS = 4
STATIONS = 512
WINDOWS = 64


def with_ends(entries, rng, smallest, top_value):
    longest = entries.shape.index(max(entries.shape))
    spots = []
    for shift in (0, 1):
        where = [jax.random.randint(jax.random.fold_in(rng, axis), (), 0, length) for axis, length in enumerate(entries.shape)]
        where[longest] = (where[longest] + shift) % entries.shape[longest]
        spots.append(tuple(where))
    return entries.at[spots[0]].set(smallest).at[spots[1]].set(top_value)


def block_scale(rng, shape, pieces, low, top_value):
    loudness = 1.0
    for dim, shards_of in pieces:
        steps = jax.random.uniform(jax.random.fold_in(jax.random.fold_in(rng, 6), dim), (shards_of,), jnp.float32, low / len(pieces), top_value / len(pieces))
        loudness = loudness * jnp.repeat(jnp.exp(steps), shape[dim] // shards_of).reshape((-1,) + (1,) * (len(shape) - 1 - dim))
    return loudness


def bell_draw(rng, extent, width, reach, cuts=(), held_as=jnp.bfloat16):
    result = jax.random.normal(rng, extent, jnp.float32) * width
    if len(cuts) > 0:
        result = block_scale(rng, extent, cuts, -0.22, 0.18) * result
    return jnp.clip(result, min=-reach, max=reach).astype(held_as)


def setup_inputs(seed: int = 0) -> dict:
    key_list = jax.random.split(jax.random.key(seed), 3)
    return {
        "spectra": bell_draw(key_list[0], (2, WINDOWS, STATIONS, F), 1.0, 6.0, ((1, 2), (2, 16)), jnp.float32),
        "valid": with_ends((jax.random.randint(key_list[1], (WINDOWS, STATIONS), 0, 4) < 3).astype(jnp.int32), jax.random.fold_in(key_list[1], 1), 0, 1),
    }


def whiten_all(spectra, valid):
    power = lax.optimization_barrier(jnp.mean(spectra[0] * spectra[0] + spectra[1] * spectra[1], axis=-1, keepdims=True))
    scale = valid.astype(jnp.float32)[..., None] / jnp.sqrt(power + 1e-06)
    return spectra * scale[None]

def reference(spectra, valid):
    whitened = whiten_all(spectra, valid)
    nblocks = STATIONS // STA_DEV
    windows = spectra.shape[1]
    own = whitened.reshape(2, windows, nblocks, STA_DEV, F)
    flipped = jnp.stack((own[1], -own[0]))
    outputs = []
    for k in range(OFFSETS):
        other = jnp.roll(whitened, -k * STA_DEV, axis=2).reshape(2, windows, nblocks, STA_DEV, F)
        real_part = jnp.einsum('cwnaf,cwnbf->nabf', own, other, precision=lax.Precision.HIGHEST)
        imag_part = jnp.einsum('cwnaf,cwnbf->nabf', flipped, other, precision=lax.Precision.HIGHEST)
        outputs.append(jnp.stack((real_part, imag_part)).reshape(2, STATIONS, STA_DEV, F) / WINDOWS)
    return jnp.stack(outputs, axis=1)
```

```python
import functools

import jax
import jax.numpy as jnp
from jax import lax
from jax.experimental import pallas as pl
from jax.experimental.pallas import tpu as pltpu
from jax.sharding import PartitionSpec as P

OFFSETS = 4
LANES = 128
ROWS = 4


def passed_along(value, axis, steps):
    count = lax.axis_size(axis)
    pairs = [(source, (source + steps) % count) for source in range(count)]
    return lax.ppermute(value, axis, pairs)


def whiten_local(spectra, valid):
    power = jnp.mean(spectra[0] * spectra[0] + spectra[1] * spectra[1], axis=-1, keepdims=True)
    scale = valid.astype(jnp.float32)[..., None] / jnp.sqrt(power + 1e-06)
    return spectra * scale[None]


def by_bins(whitened):
    chans, wins, stats, bins = whitened.shape
    return jnp.transpose(whitened, (3, 0, 1, 2)).reshape(bins, chans * wins, stats)


def cross_block(own, flipped, other, windows):
    real_part = jnp.einsum("fka,fkb->fab", own, other, precision=lax.Precision.HIGHEST)
    imag_part = jnp.einsum("fka,fkb->fab", flipped, other, precision=lax.Precision.HIGHEST)
    both = jnp.stack((real_part, imag_part)) / windows
    return jnp.transpose(both, (0, 2, 3, 1))


def on_device_general(spectra, valid):
    whitened = whiten_local(spectra, valid)
    windows = spectra.shape[1] * lax.axis_size("tm")
    own = by_bins(whitened)
    flipped = by_bins(jnp.stack((whitened[1], -whitened[0])))
    moving = own
    pieces = []
    for k in range(OFFSETS):
        if k == 0:
            other = own
        else:
            moving = passed_along(moving, "sta", -1)
            other = moving
        pieces.append(cross_block(own, flipped, other, windows))
    stacked = jnp.stack(pieces, axis=1)
    return lax.psum_scatter(stacked, "tm", scatter_dimension=3, tiled=True)


def kernel(count, chunks, spectra, valid, out, own, oth, ysend, yrecv, ssend, orecv):
    wins, stats, bins = spectra.shape[1:]
    half = stats // 2
    step = wins // chunks
    n = lax.axis_index("sta")
    t = lax.axis_index("tm")
    core = lax.rem(n, 2)
    odd = lax.rem(lax.div(n, 2), 2)
    inverse = 1.0 / (wins * 2)

    def around(by):
        return lax.rem(n + (by + count), count)

    barrier = pltpu.get_barrier_semaphore()
    pl.semaphore_signal(barrier, inc=1, device_id={"tm": 1 - t}, device_id_type=pl.DeviceIdType.MESH)
    for by in (-3, -2, -1, 1, 2, 3):
        pl.semaphore_signal(barrier, inc=1, device_id={"sta": around(by)}, device_id_type=pl.DeviceIdType.MESH)

    def span(j):
        return pl.ds(j * step, step)

    def y_copy(flow, j):
        h = 1 - t if flow == 0 else t
        return pltpu.make_async_remote_copy(
            src_ref=own.at[h, 0, :, span(j)], dst_ref=own.at[h, 1, :, span(j)],
            send_sem=ysend.at[flow, j], recv_sem=yrecv.at[flow, j],
            device_id={"tm": 1 - t}, device_id_type=pl.DeviceIdType.MESH)

    def y_wait(flow, j):
        h = t if flow == 0 else 1 - t
        pltpu.make_async_remote_copy(
            src_ref=own.at[h, 0, :, span(j)], dst_ref=own.at[h, 1, :, span(j)],
            send_sem=ysend.at[flow, j], recv_sem=yrecv.at[flow, j],
            device_id={"tm": 1 - t}, device_id_type=pl.DeviceIdType.MESH).wait_recv()

    def s_copy(flow, src, dst_k, s, j, dest):
        i = s * chunks + j
        return pltpu.make_async_remote_copy(
            src_ref=src, dst_ref=oth.at[dst_k, s, :, span(j)],
            send_sem=ssend.at[flow, i], recv_sem=orecv.at[dst_k, i],
            device_id={"sta": dest}, device_id_type=pl.DeviceIdType.MESH)

    near = around(1 - 2 * core)

    def direct_a(s, j):
        return s_copy(0, own.at[t, s, :, span(j)], 2 - 2 * core, s, j, around(2 * core - 3))

    def direct_b(s, j):
        return s_copy(1, own.at[t, s, :, span(j)], 1, s, j, around(-2))

    def relay_two(s, j):
        return s_copy(2, oth.at[1, s, :, span(j)], 2 * core, s, j, near)

    def relay_three(s, j):
        return s_copy(3, oth.at[2, s, :, span(j)], 1, s, j, around(1))

    sends_b = jnp.logical_or(core == 1, odd == 1)
    relays_three = jnp.logical_and(core == 1, odd == 0)
    late_two = jnp.logical_and(core == 0, odd == 1)

    def o_wait(k, s, j):
        s_copy(0, oth.at[k, s, :, span(j)], k, s, j, near).wait_recv()

    def direct(s, j):
        direct_a(s, j).start()

        @pl.when(sends_b)
        def _():
            direct_b(s, j).start()

    same = lax.broadcasted_iota(jnp.int32, (stats, stats), 0) == lax.broadcasted_iota(jnp.int32, (stats, stats), 1)

    def whiten(w, carry):
        re, im = spectra[0, w], spectra[1, w]
        power = jnp.mean(re * re + im * im, axis=-1, keepdims=True)
        row = valid[pl.ds(w, 1), :].astype(jnp.float32)
        column = jnp.sum(jnp.where(same, row, 0.0), axis=-1, keepdims=True)
        scale = column / jnp.sqrt(power + 1e-06)
        for c, part in enumerate((re, im)):
            part = part * scale
            for h in range(2):
                own[h, 0, c, w] = part[h * half:(h + 1) * half]
        return carry

    lax.fori_loop(0, step, whiten, 0, unroll=2)
    pl.semaphore_wait(barrier, 7)

    def first(j, carry):
        @pl.when(j + 1 < chunks)
        def _():
            lax.fori_loop((j + 1) * step, (j + 2) * step, whiten, 0)
        y_copy(0, j).start()
        direct(0, j)
        return carry

    lax.fori_loop(0, chunks, first, 0)

    def second(j, carry):
        y_copy(1, j).start()
        return carry

    lax.fori_loop(0, chunks, second, 0)

    def clear(r, carry):
        out[0, :, r] = jnp.zeros_like(out[0, :, r])
        out[1, :, r] = jnp.zeros_like(out[1, :, r])
        return carry

    lax.fori_loop(0, stats, clear, 0)

    def unit(other, k, s, j):
        last = jnp.logical_and(s == 1, j == chunks - 1)
        factor = jnp.where(last, inverse, 1.0)

        def block(p, carry):
            h = lax.div(p, bins // LANES)
            lanes = pl.ds(pl.multiple_of(lax.rem(p, bins // LANES) * LANES, LANES), LANES)
            for r0 in range(0, half, ROWS):
                a0 = h * half + r0
                total = [[out[ri, k, a0 + r, :, lanes] for ri in range(2)] for r in range(ROWS)]
                for v in range(step):
                    w = j * step + v
                    pr, pi = other(0, w, lanes), other(1, w, lanes)
                    for r in range(ROWS):
                        re = own[h, s, 0, w, r0 + r:r0 + r + 1, lanes]
                        im = own[h, s, 1, w, r0 + r:r0 + r + 1, lanes]
                        total[r][0] = total[r][0] + re * pr + im * pi
                        total[r][1] = total[r][1] + im * pr - re * pi
                for r in range(ROWS):
                    for ri in range(2):
                        out[ri, k, a0 + r, :, lanes] = total[r][ri] * factor
            return carry

        lax.fori_loop(0, 2 * (bins // LANES), block, 0)

    def zero_unit(s, j):
        unit(lambda c, w, lanes: own[t, s, c, w, :, lanes], 0, s, j)

    def other_units(s, j):
        def each(k, carry):
            unit(lambda c, w, lanes: oth[k, s, c, w, :, lanes], k + 1, s, j)
            return carry
        lax.fori_loop(0, OFFSETS - 1, each, 0)

    def zero_first(j, carry):
        zero_unit(0, j)
        return carry

    lax.fori_loop(0, chunks, zero_first, 0)

    def pulse(i, carry):
        @pl.when(i < chunks)
        def _():
            y_wait(0, i)
            direct(1, i)

        @pl.when(i < 2 * chunks)
        def _():
            s, j = lax.div(i, chunks), lax.rem(i, chunks)

            @pl.when(core == 1)
            def _():
                o_wait(2, s, j)

            @pl.when(relays_three)
            def _():
                relay_three(s, j).start()

            @pl.when(jnp.logical_not(late_two))
            def _():
                o_wait(1, s, j)
                relay_two(s, j).start()

        @pl.when(i >= 1)
        def _():
            s, j = lax.div(i - 1, chunks), lax.rem(i - 1, chunks)

            @pl.when(late_two)
            def _():
                o_wait(1, s, j)
                relay_two(s, j).start()

            @pl.when(s == 1)
            def _():
                y_wait(1, j)
                zero_unit(s, j)

            o_wait(0, s, j)

            @pl.when(core == 0)
            def _():
                o_wait(2, s, j)

            other_units(s, j)
        return carry

    lax.fori_loop(0, 2 * chunks + 1, pulse, 0)

    def drain(i, carry):
        s, j = lax.div(i, chunks), lax.rem(i, chunks)
        direct_a(s, j).wait_send()
        relay_two(s, j).wait_send()

        @pl.when(sends_b)
        def _():
            direct_b(s, j).wait_send()

        @pl.when(relays_three)
        def _():
            relay_three(s, j).wait_send()

        @pl.when(s == 0)
        def _():
            y_copy(0, j).wait_send()
            y_copy(1, j).wait_send()
        return carry

    lax.fori_loop(0, 2 * chunks, drain, 0)


def on_device(count, chunks, spectra, valid):
    wins, stats, bins = spectra.shape[1:]
    half = stats // 2
    return pl.pallas_call(
        functools.partial(kernel, count, chunks),
        out_shape=jax.ShapeDtypeStruct((2, OFFSETS, stats, half, bins), jnp.float32),
        in_specs=[pl.BlockSpec(memory_space=pltpu.VMEM)] * 2,
        out_specs=pl.BlockSpec(memory_space=pltpu.VMEM),
        scratch_shapes=[
            pltpu.VMEM((2, 2, 2, wins, half, bins), jnp.float32),
            pltpu.VMEM((OFFSETS - 1, 2, 2, wins, half, bins), jnp.float32),
            pltpu.SemaphoreType.DMA((2, chunks)),
            pltpu.SemaphoreType.DMA((2, chunks)),
            pltpu.SemaphoreType.DMA((4, 2 * chunks)),
            pltpu.SemaphoreType.DMA((OFFSETS - 1, 2 * chunks)),
        ],
        compiler_params=pltpu.CompilerParams(collective_id=0, has_side_effects=True),
        name="cross_stacks",
    )(spectra, valid)


def solution(mesh):
    count, slots = mesh.shape["sta"], mesh.shape["tm"]
    in_specs = (P(None, "tm", "sta", None), P("tm", "sta"))
    out_specs = P(None, None, "sta", "tm", None)

    def body(spectra, valid):
        wins, stats, bins = spectra.shape[1:]
        fits = slots == 2 and count % 4 == 0 and count >= 8
        fits = fits and wins % 8 == 0 and stats % 16 == 0 and bins % LANES == 0
        if not fits:
            return on_device_general(spectra, valid)
        return on_device(count, wins // 8, spectra, valid)

    return jax.shard_map(body, mesh=mesh, in_specs=in_specs, out_specs=out_specs, check_vma=False)
```

```python
import functools

import jax
import jax.numpy as jnp
from jax import lax
from jax.experimental import pallas as pl
from jax.experimental.pallas import tpu as pltpu
from jax.sharding import PartitionSpec as P

OFFSETS = 4
LANES = 128
ROWS = 4


def passed_along(value, axis, steps):
    count = lax.axis_size(axis)
    pairs = [(source, (source + steps) % count) for source in range(count)]
    return lax.ppermute(value, axis, pairs)


def whiten_local(spectra, valid):
    power = jnp.mean(spectra[0] * spectra[0] + spectra[1] * spectra[1], axis=-1, keepdims=True)
    scale = valid.astype(jnp.float32)[..., None] / jnp.sqrt(power + 1e-06)
    return spectra * scale[None]


def by_bins(whitened):
    chans, wins, stats, bins = whitened.shape
    return jnp.transpose(whitened, (3, 0, 1, 2)).reshape(bins, chans * wins, stats)


def cross_block(own, flipped, other, windows):
    real_part = jnp.einsum("fka,fkb->fab", own, other, precision=lax.Precision.HIGHEST)
    imag_part = jnp.einsum("fka,fkb->fab", flipped, other, precision=lax.Precision.HIGHEST)
    both = jnp.stack((real_part, imag_part)) / windows
    return jnp.transpose(both, (0, 2, 3, 1))


def on_device_general(spectra, valid):
    whitened = whiten_local(spectra, valid)
    windows = spectra.shape[1] * lax.axis_size("tm")
    own = by_bins(whitened)
    flipped = by_bins(jnp.stack((whitened[1], -whitened[0])))
    moving = own
    pieces = []
    for k in range(OFFSETS):
        if k == 0:
            other = own
        else:
            moving = passed_along(moving, "sta", -1)
            other = moving
        pieces.append(cross_block(own, flipped, other, windows))
    stacked = jnp.stack(pieces, axis=1)
    return lax.psum_scatter(stacked, "tm", scatter_dimension=3, tiled=True)


def kernel(count, chunks, spectra, valid, out, raw, own, oth, lsem, osem, ysend, yrecv, ssend, orecv):
    wins, stats, bins = spectra.shape[1:]
    half = stats // 2
    step = wins // chunks
    n = lax.axis_index("sta")
    t = lax.axis_index("tm")
    core = lax.rem(n, 2)
    odd = lax.rem(lax.div(n, 2), 2)
    inverse = 1.0 / (wins * 2)

    def around(by):
        return lax.rem(n + (by + count), count)

    barrier = pltpu.get_barrier_semaphore()
    pl.semaphore_signal(barrier, inc=1, device_id={"tm": 1 - t}, device_id_type=pl.DeviceIdType.MESH)
    for by in (-3, -2, -1, 1, 2, 3):
        pl.semaphore_signal(barrier, inc=1, device_id={"sta": around(by)}, device_id_type=pl.DeviceIdType.MESH)

    def span(j):
        return pl.ds(j * step, step)

    def y_copy(flow, j):
        h = 1 - t if flow == 0 else t
        return pltpu.make_async_remote_copy(
            src_ref=own.at[h, 0, :, span(j)], dst_ref=own.at[h, 1, :, span(j)],
            send_sem=ysend.at[flow, j], recv_sem=yrecv.at[flow, j],
            device_id={"tm": 1 - t}, device_id_type=pl.DeviceIdType.MESH)

    def y_wait(flow, j):
        h = t if flow == 0 else 1 - t
        pltpu.make_async_remote_copy(
            src_ref=own.at[h, 0, :, span(j)], dst_ref=own.at[h, 1, :, span(j)],
            send_sem=ysend.at[flow, j], recv_sem=yrecv.at[flow, j],
            device_id={"tm": 1 - t}, device_id_type=pl.DeviceIdType.MESH).wait_recv()

    def s_copy(flow, src, dst_k, s, j, dest):
        i = s * chunks + j
        return pltpu.make_async_remote_copy(
            src_ref=src, dst_ref=oth.at[dst_k, s, :, span(j)],
            send_sem=ssend.at[flow, i], recv_sem=orecv.at[dst_k, i],
            device_id={"sta": dest}, device_id_type=pl.DeviceIdType.MESH)

    near = around(1 - 2 * core)

    def direct_a(s, j):
        return s_copy(0, own.at[t, s, :, span(j)], 2 - 2 * core, s, j, around(2 * core - 3))

    def direct_b(s, j):
        return s_copy(1, own.at[t, s, :, span(j)], 1, s, j, around(-2))

    def relay_two(s, j):
        return s_copy(2, oth.at[1, s, :, span(j)], 2 * core, s, j, near)

    def relay_three(s, j):
        return s_copy(3, oth.at[2, s, :, span(j)], 1, s, j, around(1))

    sends_b = jnp.logical_or(core == 1, odd == 1)
    relays_three = jnp.logical_and(core == 1, odd == 0)
    late_two = jnp.logical_and(core == 0, odd == 1)

    def o_wait(k, s, j):
        s_copy(0, oth.at[k, s, :, span(j)], k, s, j, near).wait_recv()

    def direct(s, j):
        direct_a(s, j).start()

        @pl.when(sends_b)
        def _():
            direct_b(s, j).start()

    same = lax.broadcasted_iota(jnp.int32, (stats, stats), 0) == lax.broadcasted_iota(jnp.int32, (stats, stats), 1)

    def load(j):
        return pltpu.make_async_copy(spectra.at[:, span(j)], raw.at[:, span(j)], lsem.at[j])

    def whiten(j):
        load(j).wait()
        for v in range(step):
            w = j * step + v
            re, im = raw[0, w], raw[1, w]
            power = jnp.mean(re * re + im * im, axis=-1, keepdims=True)
            row = valid[pl.ds(w, 1), :].astype(jnp.float32)
            column = jnp.sum(jnp.where(same, row, 0.0), axis=-1, keepdims=True)
            scale = column / jnp.sqrt(power + 1e-06)
            for c, part in enumerate((re, im)):
                part = part * scale
                for h in range(2):
                    own[h, 0, c, w] = part[h * half:(h + 1) * half]

    def fetch(j, carry):
        load(j).start()
        return carry

    lax.fori_loop(0, chunks, fetch, 0)
    whiten(0)
    pl.semaphore_wait(barrier, 7)

    def first(j, carry):
        @pl.when(j + 1 < chunks)
        def _():
            whiten(j + 1)
        y_copy(0, j).start()
        direct(0, j)
        return carry

    lax.fori_loop(0, chunks, first, 0)

    def second(j, carry):
        y_copy(1, j).start()
        return carry

    lax.fori_loop(0, chunks, second, 0)

    def clear(r, carry):
        out[0, :, r] = jnp.zeros_like(out[0, :, r])
        out[1, :, r] = jnp.zeros_like(out[1, :, r])
        return carry

    lax.fori_loop(0, stats, clear, 0)

    def unit(other, k, s, j):
        last = jnp.logical_and(s == 1, j == chunks - 1)
        factor = jnp.where(last, inverse, 1.0)

        def block(p, carry):
            h = lax.div(p, bins // LANES)
            lanes = pl.ds(pl.multiple_of(lax.rem(p, bins // LANES) * LANES, LANES), LANES)
            for r0 in range(0, half, ROWS):
                a0 = h * half + r0
                total = [[out[ri, k, a0 + r, :, lanes] for ri in range(2)] for r in range(ROWS)]
                for v in range(step):
                    w = j * step + v
                    pr, pi = other(0, w, lanes), other(1, w, lanes)
                    for r in range(ROWS):
                        re = own[h, s, 0, w, r0 + r:r0 + r + 1, lanes]
                        im = own[h, s, 1, w, r0 + r:r0 + r + 1, lanes]
                        total[r][0] = total[r][0] + re * pr + im * pi
                        total[r][1] = total[r][1] + im * pr - re * pi
                for r in range(ROWS):
                    for ri in range(2):
                        out[ri, k, a0 + r, :, lanes] = total[r][ri] * factor
            return carry

        lax.fori_loop(0, 2 * (bins // LANES), block, 0)

    def leave(k):
        return pltpu.make_async_copy(out.at[:, k], result.at[:, k], osem.at[k])

    def emit(k, s, j):
        @pl.when(jnp.logical_and(s == 1, j == chunks - 1))
        def _():
            pass

    def zero_unit(s, j):
        unit(lambda c, w, lanes: own[t, s, c, w, :, lanes], 0, s, j)

    def other_units(s, j):
        def each(k, carry):
            unit(lambda c, w, lanes: oth[k, s, c, w, :, lanes], k + 1, s, j)
            emit(k + 1, s, j)
            return carry
        lax.fori_loop(0, OFFSETS - 1, each, 0)

    def zero_first(j, carry):
        zero_unit(0, j)
        return carry

    lax.fori_loop(0, chunks, zero_first, 0)

    def pulse(i, carry):
        @pl.when(i < chunks)
        def _():
            y_wait(0, i)
            direct(1, i)

        @pl.when(i < 2 * chunks)
        def _():
            s, j = lax.div(i, chunks), lax.rem(i, chunks)

            @pl.when(core == 1)
            def _():
                o_wait(2, s, j)

            @pl.when(relays_three)
            def _():
                relay_three(s, j).start()

            @pl.when(jnp.logical_not(late_two))
            def _():
                o_wait(1, s, j)
                relay_two(s, j).start()

        @pl.when(i >= 1)
        def _():
            s, j = lax.div(i - 1, chunks), lax.rem(i - 1, chunks)

            @pl.when(late_two)
            def _():
                o_wait(1, s, j)
                relay_two(s, j).start()

            @pl.when(s == 1)
            def _():
                y_wait(1, j)
                zero_unit(s, j)
                emit(0, s, j)

            o_wait(0, s, j)

            @pl.when(core == 0)
            def _():
                o_wait(2, s, j)

            other_units(s, j)
        return carry

    lax.fori_loop(0, 2 * chunks + 1, pulse, 0)

    def drain(i, carry):
        s, j = lax.div(i, chunks), lax.rem(i, chunks)
        direct_a(s, j).wait_send()
        relay_two(s, j).wait_send()

        @pl.when(sends_b)
        def _():
            direct_b(s, j).wait_send()

        @pl.when(relays_three)
        def _():
            relay_three(s, j).wait_send()

        @pl.when(s == 0)
        def _():
            y_copy(0, j).wait_send()
            y_copy(1, j).wait_send()
        return carry

    lax.fori_loop(0, 2 * chunks, drain, 0)

    for k in range(OFFSETS):
        pass


def on_device(count, chunks, spectra, valid):
    wins, stats, bins = spectra.shape[1:]
    half = stats // 2
    return pl.pallas_call(
        functools.partial(kernel, count, chunks),
        out_shape=jax.ShapeDtypeStruct((2, OFFSETS, stats, half, bins), jnp.float32),
        in_specs=[pl.BlockSpec(memory_space=pltpu.HBM), pl.BlockSpec(memory_space=pltpu.VMEM)],
        out_specs=pl.BlockSpec(memory_space=pltpu.VMEM),
        scratch_shapes=[
            pltpu.VMEM((2, wins, stats, bins), jnp.float32),
            pltpu.VMEM((2, 2, 2, wins, half, bins), jnp.float32),
            pltpu.VMEM((OFFSETS - 1, 2, 2, wins, half, bins), jnp.float32),
            pltpu.SemaphoreType.DMA((chunks,)),
            pltpu.SemaphoreType.DMA((OFFSETS,)),
            pltpu.SemaphoreType.DMA((2, chunks)),
            pltpu.SemaphoreType.DMA((2, chunks)),
            pltpu.SemaphoreType.DMA((4, 2 * chunks)),
            pltpu.SemaphoreType.DMA((OFFSETS - 1, 2 * chunks)),
        ],
        compiler_params=pltpu.CompilerParams(
            collective_id=0, has_side_effects=True, vmem_limit_bytes=24 * 1024 * 1024),
        name="cross_stacks",
    )(spectra, valid)


def solution(mesh):
    count, slots = mesh.shape["sta"], mesh.shape["tm"]
    in_specs = (P(None, "tm", "sta", None), P("tm", "sta"))
    out_specs = P(None, None, "sta", "tm", None)

    def body(spectra, valid):
        wins, stats, bins = spectra.shape[1:]
        fits = slots == 2 and count % 4 == 0 and count >= 8
        fits = fits and wins % 8 == 0 and stats % 16 == 0 and bins % LANES == 0
        if not fits:
            return on_device_general(spectra, valid)
        return on_device(count, wins // 4, spectra, valid)

    return jax.shard_map(body, mesh=mesh, in_specs=in_specs, out_specs=out_specs, check_vma=False)
```

```python
import functools

import jax
import jax.numpy as jnp
from jax import lax
from jax.experimental import pallas as pl
from jax.experimental.pallas import tpu as pltpu
from jax.sharding import PartitionSpec as P

OFFSETS = 4
LANES = 128
ROWS = 4


def passed_along(value, axis, steps):
    count = lax.axis_size(axis)
    pairs = [(source, (source + steps) % count) for source in range(count)]
    return lax.ppermute(value, axis, pairs)


def whiten_local(spectra, valid):
    power = jnp.mean(spectra[0] * spectra[0] + spectra[1] * spectra[1], axis=-1, keepdims=True)
    scale = valid.astype(jnp.float32)[..., None] / jnp.sqrt(power + 1e-06)
    return spectra * scale[None]


def by_bins(whitened):
    chans, wins, stats, bins = whitened.shape
    return jnp.transpose(whitened, (3, 0, 1, 2)).reshape(bins, chans * wins, stats)


def cross_block(own, flipped, other, windows):
    real_part = jnp.einsum("fka,fkb->fab", own, other, precision=lax.Precision.HIGHEST)
    imag_part = jnp.einsum("fka,fkb->fab", flipped, other, precision=lax.Precision.HIGHEST)
    both = jnp.stack((real_part, imag_part)) / windows
    return jnp.transpose(both, (0, 2, 3, 1))


def on_device_general(spectra, valid):
    whitened = whiten_local(spectra, valid)
    windows = spectra.shape[1] * lax.axis_size("tm")
    own = by_bins(whitened)
    flipped = by_bins(jnp.stack((whitened[1], -whitened[0])))
    moving = own
    pieces = []
    for k in range(OFFSETS):
        if k == 0:
            other = own
        else:
            moving = passed_along(moving, "sta", -1)
            other = moving
        pieces.append(cross_block(own, flipped, other, windows))
    stacked = jnp.stack(pieces, axis=1)
    return lax.psum_scatter(stacked, "tm", scatter_dimension=3, tiled=True)


def kernel(count, chunks, spectra, valid, out, raw, own, oth, lsem, ysend, yrecv, ssend, orecv):
    wins, stats, bins = spectra.shape[1:]
    half = stats // 2
    step = wins // chunks
    n = lax.axis_index("sta")
    t = lax.axis_index("tm")
    core = lax.rem(n, 2)
    odd = lax.rem(lax.div(n, 2), 2)
    inverse = 1.0 / (wins * 2)

    def around(by):
        return lax.rem(n + (by + count), count)

    barrier = pltpu.get_barrier_semaphore()
    pl.semaphore_signal(barrier, inc=1, device_id={"tm": 1 - t}, device_id_type=pl.DeviceIdType.MESH)
    for by in (-3, -2, -1, 1, 2, 3):
        pl.semaphore_signal(barrier, inc=1, device_id={"sta": around(by)}, device_id_type=pl.DeviceIdType.MESH)

    def span(j):
        return pl.ds(j * step, step)

    def y_copy(flow, j):
        h = 1 - t if flow == 0 else t
        return pltpu.make_async_remote_copy(
            src_ref=own.at[h, 0, :, span(j)], dst_ref=own.at[h, 1, :, span(j)],
            send_sem=ysend.at[flow, j], recv_sem=yrecv.at[flow, j],
            device_id={"tm": 1 - t}, device_id_type=pl.DeviceIdType.MESH)

    def y_wait(flow, j):
        h = t if flow == 0 else 1 - t
        pltpu.make_async_remote_copy(
            src_ref=own.at[h, 0, :, span(j)], dst_ref=own.at[h, 1, :, span(j)],
            send_sem=ysend.at[flow, j], recv_sem=yrecv.at[flow, j],
            device_id={"tm": 1 - t}, device_id_type=pl.DeviceIdType.MESH).wait_recv()

    def s_copy(flow, src, dst_k, s, j, dest):
        i = s * chunks + j
        return pltpu.make_async_remote_copy(
            src_ref=src, dst_ref=oth.at[dst_k, s, :, span(j)],
            send_sem=ssend.at[flow, i], recv_sem=orecv.at[dst_k, i],
            device_id={"sta": dest}, device_id_type=pl.DeviceIdType.MESH)

    near = around(1 - 2 * core)

    def direct_a(s, j):
        return s_copy(0, own.at[t, s, :, span(j)], 2 - 2 * core, s, j, around(2 * core - 3))

    def direct_b(s, j):
        return s_copy(1, own.at[t, s, :, span(j)], 1, s, j, around(-2))

    def relay_two(s, j):
        return s_copy(2, oth.at[1, s, :, span(j)], 2 * core, s, j, near)

    def relay_three(s, j):
        return s_copy(3, oth.at[2, s, :, span(j)], 1, s, j, around(1))

    sends_b = jnp.logical_or(core == 1, odd == 1)
    relays_three = jnp.logical_and(core == 1, odd == 0)
    late_two = jnp.logical_and(core == 0, odd == 1)

    def o_wait(k, s, j):
        s_copy(0, oth.at[k, s, :, span(j)], k, s, j, near).wait_recv()

    def direct(s, j):
        direct_a(s, j).start()

        @pl.when(sends_b)
        def _():
            direct_b(s, j).start()

    same = lax.broadcasted_iota(jnp.int32, (stats, stats), 0) == lax.broadcasted_iota(jnp.int32, (stats, stats), 1)

    def load(j):
        return pltpu.make_async_copy(spectra.at[:, span(j)], raw.at[:, span(j)], lsem.at[j])

    def whiten(j):
        load(j).wait()
        for v in range(step):
            w = j * step + v
            re, im = raw[0, w], raw[1, w]
            power = jnp.mean(re * re + im * im, axis=-1, keepdims=True)
            row = valid[pl.ds(w, 1), :].astype(jnp.float32)
            column = jnp.sum(jnp.where(same, row, 0.0), axis=-1, keepdims=True)
            scale = column / jnp.sqrt(power + 1e-06)
            for c, part in enumerate((re, im)):
                part = part * scale
                for h in range(2):
                    own[h, 0, c, w] = part[h * half:(h + 1) * half]

    def fetch(j, carry):
        load(j).start()
        return carry

    lax.fori_loop(0, chunks, fetch, 0)
    whiten(0)
    pl.semaphore_wait(barrier, 7)

    def first(j, carry):
        @pl.when(j + 1 < chunks)
        def _():
            whiten(j + 1)
        y_copy(0, j).start()
        direct(0, j)
        return carry

    lax.fori_loop(0, chunks, first, 0)

    def second(j, carry):
        y_copy(1, j).start()
        return carry

    lax.fori_loop(0, chunks, second, 0)

    def clear(r, carry):
        out[0, :, r] = jnp.zeros_like(out[0, :, r])
        out[1, :, r] = jnp.zeros_like(out[1, :, r])
        return carry

    lax.fori_loop(0, stats, clear, 0)

    def unit(other, k, s, j):
        last = jnp.logical_and(s == 1, j == chunks - 1)
        factor = jnp.where(last, inverse, 1.0)

        def block(p, carry):
            h = lax.div(p, bins // LANES)
            lanes = pl.ds(pl.multiple_of(lax.rem(p, bins // LANES) * LANES, LANES), LANES)
            for r0 in range(0, half, ROWS):
                a0 = h * half + r0
                total = [None] * ROWS
                for v in range(step):
                    w = j * step + v
                    pr, pi = other(0, w, lanes), other(1, w, lanes)
                    pd = pr - pi
                    for r in range(ROWS):
                        re = own[h, s, 0, w, r0 + r:r0 + r + 1, lanes]
                        im = own[h, s, 1, w, r0 + r:r0 + r + 1, lanes]
                        terms = (re * pr, im * pi, (re + im) * pd)
                        total[r] = terms if v == 0 else tuple(x + y for x, y in zip(total[r], terms))
                for r in range(ROWS):
                    first_term, second_term, third_term = total[r]
                    pair = (first_term + second_term, third_term - first_term + second_term)
                    for ri in range(2):
                        out[ri, k, a0 + r, :, lanes] = (out[ri, k, a0 + r, :, lanes] + pair[ri]) * factor
            return carry

        lax.fori_loop(0, 2 * (bins // LANES), block, 0)

    def zero_unit(s, j):
        unit(lambda c, w, lanes: own[t, s, c, w, :, lanes], 0, s, j)

    def other_units(s, j):
        def each(p, carry):
            k = jnp.where(p == 0, 1, jnp.where(p == 1, 2 * core, 2 - 2 * core))

            @pl.when(jnp.logical_or(p == 2, jnp.logical_and(p == 1, core == 0)))
            def _():
                o_wait(k, s, j)

            unit(lambda c, w, lanes: oth[k, s, c, w, :, lanes], k + 1, s, j)
            return carry

        lax.fori_loop(0, OFFSETS - 1, each, 0)

    def zero_first(j, carry):
        zero_unit(0, j)
        return carry

    lax.fori_loop(0, chunks, zero_first, 0)

    def pulse(i, carry):
        @pl.when(i < chunks)
        def _():
            y_wait(0, i)
            direct(1, i)

        @pl.when(i < 2 * chunks)
        def _():
            s, j = lax.div(i, chunks), lax.rem(i, chunks)

            @pl.when(core == 1)
            def _():
                o_wait(2, s, j)

            @pl.when(relays_three)
            def _():
                relay_three(s, j).start()

            @pl.when(jnp.logical_not(late_two))
            def _():
                o_wait(1, s, j)
                relay_two(s, j).start()

        @pl.when(i >= 1)
        def _():
            s, j = lax.div(i - 1, chunks), lax.rem(i - 1, chunks)

            @pl.when(late_two)
            def _():
                o_wait(1, s, j)
                relay_two(s, j).start()

            @pl.when(s == 1)
            def _():
                y_wait(1, j)
                zero_unit(s, j)

            other_units(s, j)
        return carry

    lax.fori_loop(0, 2 * chunks + 1, pulse, 0)

    def drain(i, carry):
        s, j = lax.div(i, chunks), lax.rem(i, chunks)
        direct_a(s, j).wait_send()
        relay_two(s, j).wait_send()

        @pl.when(sends_b)
        def _():
            direct_b(s, j).wait_send()

        @pl.when(relays_three)
        def _():
            relay_three(s, j).wait_send()

        @pl.when(s == 0)
        def _():
            y_copy(0, j).wait_send()
            y_copy(1, j).wait_send()
        return carry

    lax.fori_loop(0, 2 * chunks, drain, 0)


def on_device(count, chunks, spectra, valid):
    wins, stats, bins = spectra.shape[1:]
    half = stats // 2
    return pl.pallas_call(
        functools.partial(kernel, count, chunks),
        out_shape=jax.ShapeDtypeStruct((2, OFFSETS, stats, half, bins), jnp.float32),
        in_specs=[pl.BlockSpec(memory_space=pltpu.HBM), pl.BlockSpec(memory_space=pltpu.VMEM)],
        out_specs=pl.BlockSpec(memory_space=pltpu.VMEM),
        scratch_shapes=[
            pltpu.VMEM((2, wins, stats, bins), jnp.float32),
            pltpu.VMEM((2, 2, 2, wins, half, bins), jnp.float32),
            pltpu.VMEM((OFFSETS - 1, 2, 2, wins, half, bins), jnp.float32),
            pltpu.SemaphoreType.DMA((chunks,)),
            pltpu.SemaphoreType.DMA((2, chunks)),
            pltpu.SemaphoreType.DMA((2, chunks)),
            pltpu.SemaphoreType.DMA((4, 2 * chunks)),
            pltpu.SemaphoreType.DMA((OFFSETS - 1, 2 * chunks)),
        ],
        compiler_params=pltpu.CompilerParams(
            collective_id=0, has_side_effects=True, vmem_limit_bytes=24 * 1024 * 1024),
        name="cross_stacks",
    )(spectra, valid)


def solution(mesh):
    count, slots = mesh.shape["sta"], mesh.shape["tm"]
    in_specs = (P(None, "tm", "sta", None), P("tm", "sta"))
    out_specs = P(None, None, "sta", "tm", None)

    def body(spectra, valid):
        wins, stats, bins = spectra.shape[1:]
        fits = slots == 2 and count % 4 == 0 and count >= 8
        fits = fits and wins % 8 == 0 and stats % 16 == 0 and bins % LANES == 0
        if not fits:
            return on_device_general(spectra, valid)
        return on_device(count, wins // 4, spectra, valid)

    return jax.shard_map(body, mesh=mesh, in_specs=in_specs, out_specs=out_specs, check_vma=False)
```
